128 devices in a mesh: dp: 16 (over z, y), ctx: 8 (over x, core).
Axes of the slice: x: 4, y: 4, z: 4, core: 2. Of those that a mesh axis runs over, the one named last changes fastest.
Arguments:
- hidden_in: bfloat16 [16384, 960], P(('dp', 'ctx')), may hold values from -6 to 6
- out_grad: bfloat16 [16384, 960], P(('dp', 'ctx')), may hold values from -6 to 6
- norm_gains: bfloat16 [2, 960], P(None, 'dp'), may hold values from 0.5 to 1.5
- q_weight: bfloat16 [960, 960], P('dp'), may hold values from -0.1875 to 0.1875
- k_weight: bfloat16 [960, 320], P('dp'), may hold values from -0.1875 to 0.1875
- v_weight: bfloat16 [960, 320], P('dp'), may hold values from -0.1875 to 0.1875
- out_weight: bfloat16 [960, 960], P('dp'), may hold values from -0.75 to 0.75
- gate_weight: bfloat16 [960, 2560], P('dp'), may hold values from -0.1875 to 0.1875
- up_weight: bfloat16 [960, 2560], P('dp'), may hold values from -0.1875 to 0.1875
- down_weight: bfloat16 [960, 2560], P('dp'), may hold values from -0.125 to 0.125
Outputs:
- hidden_out: bfloat16 [16384, 960], P(('dp', 'ctx'))
- in_grad: float32 [16384, 960], P(('dp', 'ctx'))
- gains_grad: float32 [2, 960], P(None, 'dp')
- q_weight_grad: float32 [960, 960], P('dp')
- k_weight_grad: float32 [960, 320], P('dp')
- v_weight_grad: float32 [960, 320], P('dp')
- out_weight_grad: float32 [960, 960], P('dp')
- gate_weight_grad: float32 [960, 2560], P('dp')
- up_weight_grad: float32 [960, 2560], P('dp')
- down_weight_grad: float32 [960, 2560], P('dp')
The draws below stay inside these ranges and needn't reach their ends.
All inputs are finite; a program needn't handle non-finite values.
Results may differ from the reference program's by a relative error of at most 0.015.
Values may be sent and summed in bfloat16 or wider, within the bound.
No kernel may reach another device: no remote copies, remote signals or barrier semaphores. Data moves between devices by JAX's collectives and lax.ppermute only.
A program may use at most 192 MiB of HBM per device.

```python
import math
import jax
import jax.numpy as jnp
from jax import lax

D = 960
HEADS = 15
KV_HEADS = 5
HEAD_DIM = 64
FF = 2560
LEN = 1024
SEQS = 16
TOKENS = 16384


def block_scale(rng, shape, split, least, largest):
    level, own = 1.0, jax.random.fold_in(rng, 6)
    for dim, blocks in split:
        heights = jnp.exp(jax.random.uniform(jax.random.fold_in(own, dim), (blocks,), jnp.float32, least / len(split), largest / len(split)))
        level = level * jnp.repeat(heights, shape[dim] // blocks).reshape([-1 if axis == dim else 1 for axis in range(len(shape))])
    return level


def centred(own_key, extent, width, reach, cuts=(), kind=jnp.bfloat16):
    level = block_scale(own_key, extent, cuts, -0.22, 0.18) if cuts else 1.0
    values = jax.random.normal(own_key, extent, jnp.float32) * width * level
    return jnp.minimum(jnp.maximum(values, -reach), reach).astype(kind)


def setup_inputs(seed: int = 0) -> dict:
    key_list = jax.random.split(jax.random.key(seed), 11)
    return {
        "hidden_in": centred(key_list[0], (TOKENS, D), 1.0, 6.0, ((0, 128),)),
        "out_grad": centred(key_list[1], (TOKENS, D), 1.0, 6.0, ((0, 128),)),
        "norm_gains": jnp.clip(1.0 + 0.1 * jax.random.normal(key_list[2], (2, D), jnp.float32), 0.5, 1.5).astype(jnp.bfloat16),
        "q_weight": centred(key_list[3], (D, HEADS * HEAD_DIM), D ** -0.5, 0.1875, ((0, 16),)),
        "k_weight": centred(key_list[4], (D, KV_HEADS * HEAD_DIM), D ** -0.5, 0.1875, ((0, 16),)),
        "v_weight": centred(key_list[5], (D, KV_HEADS * HEAD_DIM), D ** -0.5, 0.1875, ((0, 16),)),
        "out_weight": centred(key_list[6], (D, HEADS * HEAD_DIM), (HEADS * HEAD_DIM // 16) ** -0.5, 0.75, ((0, 16),)),
        "gate_weight": centred(key_list[7], (D, FF), D ** -0.5, 0.1875, ((0, 16),)),
        "up_weight": centred(key_list[8], (D, FF), D ** -0.5, 0.1875, ((0, 16),)),
        "down_weight": centred(key_list[9], (D, FF), FF ** -0.5, 0.125, ((0, 16),)),
    }


EPS = 1e-05
ROPE_BASE = 100000.0
NEG_FILL = -1e+30

def rotary(positions, head_size):
    half = head_size // 2
    freq = ROPE_BASE ** (-(jnp.arange(half, dtype=jnp.float32) * 2.0) / head_size)
    angles = positions[:, None] * freq[None, :]
    return (jnp.concatenate([jnp.cos(angles), jnp.cos(angles)], axis=1), jnp.concatenate([jnp.sin(angles), jnp.sin(angles)], axis=1))

def rotate(values, cosine, sine, sign):
    half = values.shape[-1] // 2
    turned = jnp.concatenate([-values[..., half:], values[..., :half]], axis=-1)
    return values * cosine[:, None, :] + sign * turned * sine[:, None, :]

def norm_forward(values):
    scale = lax.rsqrt(lax.optimization_barrier(jnp.mean(values * values, axis=1, keepdims=True)) + EPS)
    return (values * scale, scale)

def norm_backward(grad_normed, normed, scale, gain):
    weighted = grad_normed * gain
    inner = lax.optimization_barrier(jnp.mean(weighted * normed, axis=1, keepdims=True))
    return (scale * (weighted - normed * inner), lax.optimization_barrier(jnp.sum(grad_normed * normed, axis=0)))

def contract_rows(left, right):
    return lax.dot_general(left, right, (((0,), (0,)), ((), ())), preferred_element_type=jnp.float32)

def contract_cols(left, right):
    return lax.dot_general(left, right, (((1,), (1,)), ((), ())), preferred_element_type=jnp.float32)

def widen(values):
    return lax.optimization_barrier(values).astype(jnp.float32)

def attend_forward(queries, keys, values, length):
    block = min(512, length)
    count = length // block
    groups = queries.shape[2]
    scaling = 1.0 / math.sqrt(HEAD_DIM)
    key_pos = jnp.arange(length, dtype=jnp.int32)
    keys_wide = keys.astype(jnp.float32)
    values_wide = values.astype(jnp.float32)

    def one_block(start):
        block_q = lax.dynamic_slice_in_dim(queries, start, block, 0).astype(jnp.float32)
        query_pos = start + jnp.arange(block, dtype=jnp.int32)
        allowed = key_pos[None, :] <= query_pos[:, None]
        scores = jnp.where(allowed, jnp.einsum('skgd,pkd->kgsp', block_q, keys_wide) * scaling, NEG_FILL)
        peak = lax.optimization_barrier(jnp.max(scores, axis=3))
        weights = jnp.where(allowed, jnp.exp(scores - peak[..., None]), 0.0)
        total = lax.optimization_barrier(jnp.sum(weights, axis=3))
        summed = jnp.einsum('kgsp,pkd->skgd', widen(weights.astype(jnp.bfloat16)), values_wide)
        result = (summed / jnp.transpose(total, (2, 0, 1))[..., None]).astype(jnp.bfloat16)
        return (result, jnp.transpose(peak + jnp.log(total), (2, 0, 1)))
    starts = jnp.arange(count, dtype=jnp.int32) * block
    results, lses = lax.map(one_block, starts)
    return (results.reshape(length, HEADS * HEAD_DIM), lses.reshape(length, KV_HEADS, groups))

def attend_backward(queries, keys, values, grads, lse, delta, length):
    block = min(512, length)
    count = length // block
    scaling = 1.0 / math.sqrt(HEAD_DIM)
    key_pos = jnp.arange(length, dtype=jnp.int32)
    keys_wide = keys.astype(jnp.float32)
    values_wide = values.astype(jnp.float32)

    def one_block(carry, start):
        key_acc, value_acc = carry
        block_q = lax.dynamic_slice_in_dim(queries, start, block, 0).astype(jnp.float32)
        block_g = lax.dynamic_slice_in_dim(grads, start, block, 0).astype(jnp.float32)
        block_lse = jnp.transpose(lax.dynamic_slice_in_dim(lse, start, block, 0), (1, 2, 0))
        block_delta = jnp.transpose(lax.dynamic_slice_in_dim(delta, start, block, 0), (1, 2, 0))
        query_pos = start + jnp.arange(block, dtype=jnp.int32)
        allowed = key_pos[None, :] <= query_pos[:, None]
        scores = jnp.einsum('skgd,pkd->kgsp', block_q, keys_wide) * scaling
        probs = jnp.exp(jnp.where(allowed, scores - block_lse[..., None], NEG_FILL))
        value_acc = value_acc + jnp.einsum('kgsp,skgd->pkd', widen(probs.astype(jnp.bfloat16)), block_g)
        prob_grad = jnp.einsum('skgd,pkd->kgsp', block_g, values_wide)
        score_grad = (probs * (prob_grad - block_delta[..., None]) * scaling).astype(jnp.bfloat16)
        score_wide = widen(score_grad)
        query_grad = jnp.einsum('kgsp,pkd->skgd', score_wide, keys_wide)
        key_acc = key_acc + jnp.einsum('kgsp,skgd->pkd', score_wide, block_q)
        return ((key_acc, value_acc), query_grad)
    empty = jnp.zeros((length, KV_HEADS, HEAD_DIM), jnp.float32)
    starts = jnp.arange(count, dtype=jnp.int32) * block
    (key_acc, value_acc), query_grads = lax.scan(one_block, (empty, empty), starts)
    return (query_grads.reshape(length, HEADS, HEAD_DIM), key_acc, value_acc)

def reference(hidden_in, out_grad, norm_gains, q_weight, k_weight, v_weight, out_weight, gate_weight, up_weight, down_weight):
    groups = HEADS // KV_HEADS
    kv_width = KV_HEADS * HEAD_DIM
    gain_first = norm_gains[0].astype(jnp.float32)
    gain_second = norm_gains[1].astype(jnp.float32)
    cosine, sine = rotary(jnp.arange(LEN, dtype=jnp.float32), HEAD_DIM)

    def one_sequence(carry, inputs):
        tokens_in, cotangent = inputs
        inputs_wide = tokens_in.astype(jnp.float32)
        normed_one, scale_one = norm_forward(inputs_wide)
        first_in = (normed_one * gain_first).astype(jnp.bfloat16)
        queries = jnp.dot(first_in, q_weight, preferred_element_type=jnp.float32).reshape(LEN, HEADS, HEAD_DIM)
        queries = rotate(queries, cosine, sine, 1.0).astype(jnp.bfloat16).reshape(LEN, KV_HEADS, groups, HEAD_DIM)
        keys = jnp.dot(first_in, k_weight, preferred_element_type=jnp.float32).reshape(LEN, KV_HEADS, HEAD_DIM)
        keys = rotate(keys, cosine, sine, 1.0).astype(jnp.bfloat16)
        values = jnp.dot(first_in, v_weight, preferred_element_type=jnp.float32).astype(jnp.bfloat16)
        values = values.reshape(LEN, KV_HEADS, HEAD_DIM)
        attn, lse = attend_forward(queries, keys, values, LEN)
        middle = inputs_wide + contract_cols(attn, out_weight)
        normed_two, scale_two = norm_forward(middle)
        second_in = (normed_two * gain_second).astype(jnp.bfloat16)
        gate = jnp.dot(second_in, gate_weight, preferred_element_type=jnp.float32)
        up_part = jnp.dot(second_in, up_weight, preferred_element_type=jnp.float32)
        sigma = jax.nn.sigmoid(gate)
        hidden = (gate * sigma * up_part).astype(jnp.bfloat16)
        hidden_out = (middle + contract_cols(hidden, down_weight)).astype(jnp.bfloat16)
        grad_hidden = jnp.dot(cotangent, down_weight, preferred_element_type=jnp.float32)
        grad_gate = (grad_hidden * up_part * sigma * (1.0 + gate * (1.0 - sigma))).astype(jnp.bfloat16)
        grad_up = (grad_hidden * gate * sigma).astype(jnp.bfloat16)
        down_term = contract_rows(cotangent, hidden)
        gate_term = contract_rows(second_in, grad_gate)
        up_term = contract_rows(second_in, grad_up)
        grad_second = contract_cols(grad_gate, gate_weight) + contract_cols(grad_up, up_weight)
        back_two, gain_two_term = norm_backward(grad_second, normed_two, scale_two, gain_second)
        grad_middle = cotangent.astype(jnp.float32) + back_two
        middle_low = grad_middle.astype(jnp.bfloat16)
        output_term = contract_rows(middle_low, attn)
        grad_attn = jnp.dot(middle_low, out_weight, preferred_element_type=jnp.float32).astype(jnp.bfloat16)
        grad_heads = grad_attn.reshape(LEN, KV_HEADS, groups, HEAD_DIM)
        attn_heads = attn.reshape(LEN, KV_HEADS, groups, HEAD_DIM)
        delta = lax.optimization_barrier(jnp.sum(grad_heads.astype(jnp.float32) * attn_heads.astype(jnp.float32), axis=3))
        query_grad, key_grad, value_grad = attend_backward(queries, keys, values, grad_heads, lse, delta, LEN)
        query_low = rotate(query_grad, cosine, sine, -1.0).astype(jnp.bfloat16).reshape(LEN, HEADS * HEAD_DIM)
        key_low = rotate(key_grad, cosine, sine, -1.0).astype(jnp.bfloat16).reshape(LEN, kv_width)
        value_low = value_grad.astype(jnp.bfloat16).reshape(LEN, kv_width)
        query_term = contract_rows(first_in, query_low)
        key_term = contract_rows(first_in, key_low)
        value_term = contract_rows(first_in, value_low)
        grad_first = contract_cols(query_low, q_weight) + contract_cols(key_low, k_weight) + contract_cols(value_low, v_weight)
        back_one, gain_one_term = norm_backward(grad_first, normed_one, scale_one, gain_first)
        in_grad = grad_middle + back_one
        terms = (jnp.stack([gain_one_term, gain_two_term]), query_term, key_term, value_term, output_term, gate_term, up_term, down_term)
        new_carry = tuple((old + term for old, term in zip(carry, terms)))
        return (new_carry, (hidden_out, in_grad))
    start = (jnp.zeros((2, D), jnp.float32), jnp.zeros((D, HEADS * HEAD_DIM), jnp.float32), jnp.zeros((D, kv_width), jnp.float32), jnp.zeros((D, kv_width), jnp.float32), jnp.zeros((D, HEADS * HEAD_DIM), jnp.float32), jnp.zeros((D, FF), jnp.float32), jnp.zeros((D, FF), jnp.float32), jnp.zeros((D, FF), jnp.float32))
    totals, (outputs, in_grads) = lax.scan(one_sequence, start, (hidden_in.reshape(SEQS, LEN, D), out_grad.reshape(SEQS, LEN, D)))
    return (outputs.reshape(TOKENS, D), in_grads.reshape(TOKENS, D), totals[0], totals[1], totals[2], totals[3], totals[4], totals[5], totals[6], totals[7])
```

```python
import math

import jax
import jax.numpy as jnp
import numpy as np
from jax import lax
from jax.experimental import pallas as pl
from jax.experimental.pallas import tpu as pltpu
from jax.sharding import PartitionSpec as P

D = 960
HEADS = 15
KV_HEADS = 5
HEAD_DIM = 64
FF = 2560
EPS = 1e-05
ROPE_BASE = 100000.0
NEG_FILL = -1e30

ROWS = 60
PADDED = 64
DP = 16
SIDE = 4
CTX = 8
CHIPS = 4
TOK = 128
LEN = 1024
WIDE = DP * PADDED
FSL = FF // CTX
QB = 256

BF = jnp.bfloat16
F32 = jnp.float32
NT = (((1,), (1,)), ((), ()))
TN = (((0,), (0,)), ((), ()))
NN = (((1,), (0,)), ((), ()))


def dot(a, b, dims):
    return lax.dot_general(a, b, dims, preferred_element_type=F32)


def widen_features(v):
    rows = v.shape[0]
    v = jnp.pad(v.reshape(rows, DP, ROWS), ((0, 0), (0, 0), (0, PADDED - ROWS)))
    return v.reshape(rows, WIDE)


def narrow_features(v):
    rows = v.shape[0]
    return v.reshape(rows, DP, PADDED)[:, :, :ROWS].reshape(rows, D)


def along_x(v, d):
    return lax.ppermute(v, "ctx", [(i, (i + 2 * d) % CTX) for i in range(CTX)])


def other_core(v):
    return lax.ppermute(v, "ctx", [(i, i ^ 1) for i in range(CTX)])


def along_y(v, d):
    return lax.ppermute(
        v, "dp", [(i, (i // SIDE) * SIDE + (i + d) % SIDE) for i in range(DP)]
    )


def along_z(v, d):
    return lax.ppermute(v, "dp", [(i, (i + SIDE * d) % DP) for i in range(DP)])


def placed(pieces, first, count):
    out = jnp.zeros((count,) + pieces[0].shape, pieces[0].dtype)
    for d, piece in enumerate(pieces):
        out = lax.dynamic_update_slice_in_dim(out, piece[None], (first - d) % count, 0)
    return out


def gather_ctx(v):
    index = lax.axis_index("ctx")
    chip, core = index // 2, index % 2
    mine = placed([v] + [along_x(v, d) for d in (1, 2, 3)], chip, CHIPS)
    theirs = other_core(mine)
    both = jnp.where(core == 0, jnp.stack([mine, theirs], 1), jnp.stack([theirs, mine], 1))
    return both.reshape((CTX,) + v.shape)


def scatter_ctx(parts):
    index = lax.axis_index("ctx")
    chip, core = index // 2, index % 2
    split = parts.reshape((CHIPS, 2) + parts.shape[1:])
    keep = lax.dynamic_index_in_dim(split, core, 1, keepdims=False)
    give = lax.dynamic_index_in_dim(split, 1 - core, 1, keepdims=False)
    got = other_core(give)
    pair = (keep.astype(F32) + got.astype(F32)).astype(BF)
    total = (
        lax.dynamic_index_in_dim(keep, chip, 0, keepdims=False).astype(F32)
        + lax.dynamic_index_in_dim(got, chip, 0, keepdims=False).astype(F32)
    )
    for d in (1, 2, 3):
        block = lax.dynamic_index_in_dim(pair, (chip + d) % CHIPS, 0, keepdims=False)
        total = total + along_x(block, d).astype(F32)
    return total


def gather_yz(v):
    index = lax.axis_index("dp")
    z, y = index // SIDE, index % SIDE
    row = placed([v] + [along_y(v, d) for d in (1, 2, 3)], y, SIDE)
    full = placed([row] + [along_z(row, d) for d in (1, 2, 3)], z, SIDE)
    return full.reshape(DP * v.shape[0], v.shape[1])


def gather_zy(v):
    index = lax.axis_index("dp")
    z, y = index // SIDE, index % SIDE
    col = placed([v] + [along_z(v, d) for d in (1, 2, 3)], z, SIDE)
    full = placed([col] + [along_y(col, d) for d in (1, 2, 3)], y, SIDE)
    return jnp.swapaxes(full, 0, 1).reshape(DP * v.shape[0], v.shape[1])


def scatter_dp(v):
    got = lax.all_to_all(v.astype(BF), "dp", 0, 0, tiled=True)
    return jnp.sum(got.reshape(DP, PADDED, v.shape[1]).astype(F32), axis=0)


def turned(v):
    lane = lax.broadcasted_iota(jnp.int32, v.shape, 1)
    ahead = pltpu.roll(v, 96, 1)
    behind = pltpu.roll(v, 32, 1)
    return jnp.where(lane % 64 < 32, ahead, behind)


def head_mask(shape, head):
    lane = lax.broadcasted_iota(jnp.int32, shape, 1)
    return (lane // 64) == head


def forward_kernel(x_ref, w_ref, g_ref, cos_ref, sin_ref, h_ref, qkv_ref, attn_ref, lse_ref, vt_ref):
    gain = g_ref[...]
    for i in range(LEN // QB):
        rows = pl.ds(i * QB, QB)
        x = x_ref[rows, :].astype(F32)
        scale = lax.rsqrt(jnp.sum(x * x, axis=1, keepdims=True) * (1.0 / D) + EPS)
        h = (x * scale * gain).astype(BF)
        h_ref[rows, :] = h
        qkv = dot(h, w_ref[...], NN)
        cos, sin = cos_ref[rows, :], sin_ref[rows, :]
        q, k = qkv[:, :128], qkv[:, 128:256]
        qkv_ref[rows, 0:128] = (q * cos + turned(q) * sin).astype(BF)
        qkv_ref[rows, 128:256] = (k * cos + turned(k) * sin).astype(BF)
        v = qkv[:, 256:384].astype(BF)
        qkv_ref[rows, 256:384] = v
        vt_ref[:, i * QB : (i + 1) * QB] = v.T
    for i in range(LEN // QB):
        span = (i + 1) * QB
        q = qkv_ref[pl.ds(i * QB, QB), 0:128]
        keys = qkv_ref[pl.ds(0, span), 128:256]
        halves = []
        for head in range(2):
            qm = jnp.where(head_mask(q.shape, head), q, jnp.zeros_like(q)) * BF(0.125)
            s = dot(keys, qm, NT)
            kpos = lax.broadcasted_iota(jnp.int32, s.shape, 0)
            qpos = lax.broadcasted_iota(jnp.int32, s.shape, 1) + i * QB
            s = jnp.where(kpos <= qpos, s, NEG_FILL)
            peak = jnp.max(s, axis=0, keepdims=True)
            p = jnp.exp(s - peak)
            total = jnp.sum(p, axis=0, keepdims=True)
            o = dot(vt_ref[64 * head : 64 * head + 64, 0:span], p.astype(BF), NN)
            halves.append(o / total)
            lse_ref[head : head + 1, i * QB : (i + 1) * QB] = peak + jnp.log(total)
        attn_ref[pl.ds(i * QB, QB), :] = jnp.concatenate(halves, axis=0).T.astype(BF)


def backward_kernel(
    qkv_ref, attn_ref, lse_ref, g_ref, cos_ref, sin_ref, out_ref, kt_ref, dk_ref, dv_ref
):
    dk_ref[...] = jnp.zeros_like(dk_ref)
    dv_ref[...] = jnp.zeros_like(dv_ref)
    kt_ref[...] = qkv_ref[:, 128:256].T
    for i in range(LEN // QB):
        rows = pl.ds(i * QB, QB)
        span = (i + 1) * QB
        q = qkv_ref[rows, 0:128]
        keys = qkv_ref[pl.ds(0, span), 128:256]
        values = qkv_ref[pl.ds(0, span), 256:384]
        g = g_ref[rows, :]
        prod = (g.astype(F32) * attn_ref[rows, :].astype(F32)).T
        halves = []
        for head in range(2):
            mask = head_mask(q.shape, head)
            qm = jnp.where(mask, q, jnp.zeros_like(q))
            gm = jnp.where(mask, g, jnp.zeros_like(g))
            delta = jnp.sum(prod[64 * head : 64 * head + 64, :], axis=0, keepdims=True)
            s = dot(keys, qm * BF(0.125), NT) - lse_ref[head : head + 1, i * QB : (i + 1) * QB]
            kpos = lax.broadcasted_iota(jnp.int32, s.shape, 0)
            qpos = lax.broadcasted_iota(jnp.int32, s.shape, 1) + i * QB
            p = jnp.exp(jnp.where(kpos <= qpos, s, NEG_FILL))
            dv_ref[pl.ds(0, span), :] += dot(p.astype(BF), gm, NN)
            dp = dot(values, gm, NT)
            ds = (p * (dp - delta) * 0.125).astype(BF)
            dk_ref[pl.ds(0, span), :] += dot(ds, qm, NN)
            halves.append(dot(kt_ref[64 * head : 64 * head + 64, 0:span], ds, NN))
        dq = jnp.concatenate(halves, axis=0).T
        out_ref[rows, 0:128] = (dq * cos_ref[rows, :] - turned(dq) * sin_ref[rows, :]).astype(BF)
    dk = dk_ref[...]
    out_ref[:, 128:256] = (dk * cos_ref[...] - turned(dk) * sin_ref[...]).astype(BF)
    out_ref[:, 256:384] = dv_ref[...].astype(BF)


def attend(x, w, gain, cos, sin):
    return pl.pallas_call(
        forward_kernel,
        out_shape=(
            jax.ShapeDtypeStruct((LEN, WIDE), BF),
            jax.ShapeDtypeStruct((LEN, 384), BF),
            jax.ShapeDtypeStruct((LEN, 128), BF),
            jax.ShapeDtypeStruct((8, LEN), F32),
        ),
        scratch_shapes=[pltpu.VMEM((128, LEN), BF)],
        cost_estimate=pl.CostEstimate(
            flops=2 * LEN * WIDE * 384 + 4 * 2 * LEN * LEN * 128,
            bytes_accessed=8 << 20,
            transcendentals=2 * LEN * LEN,
        ),
        name="attend_forward",
    )(x, w, gain, cos, sin)


def attend_back(qkv, attn, lse, grad, cos, sin):
    return pl.pallas_call(
        backward_kernel,
        out_shape=jax.ShapeDtypeStruct((LEN, 384), BF),
        scratch_shapes=[
            pltpu.VMEM((128, LEN), BF),
            pltpu.VMEM((LEN, 128), F32),
            pltpu.VMEM((LEN, 128), F32),
        ],
        cost_estimate=pl.CostEstimate(
            flops=10 * 2 * LEN * LEN * 128, bytes_accessed=4 << 20, transcendentals=2 * LEN * LEN
        ),
        name="attend_backward",
    )(qkv, attn, lse, grad, cos, sin)


def rotary_tables():
    half = HEAD_DIM // 2
    freq = ROPE_BASE ** (-(jnp.arange(half, dtype=F32) * 2.0) / HEAD_DIM)
    angles = jnp.arange(LEN, dtype=F32)[:, None] * freq[None, :]
    c, s = jnp.cos(angles), jnp.sin(angles)
    return jnp.concatenate([c, c, c, c], axis=1), jnp.concatenate([-s, s, -s, s], axis=1)


def on_device(
    hidden_in,
    out_grad,
    norm_gains,
    q_weight,
    k_weight,
    v_weight,
    out_weight,
    gate_weight,
    up_weight,
    down_weight,
):
    index = lax.axis_index("ctx")

    def columns(w, start, width):
        return lax.dynamic_slice_in_dim(w, start, width, 1)

    def pad_rows(w):
        return jnp.pad(w, ((0, PADDED - ROWS), (0, 0)))

    first, second = (2 * index) // 3, jnp.minimum((2 * index + 1) // 3, KV_HEADS - 1)
    q_cols = columns(jnp.pad(q_weight, ((0, 0), (0, 64))), 128 * index, 128)
    k_cols = [columns(k_weight, 64 * j, 64) for j in (first, second)]
    v_cols = [columns(v_weight, 64 * j, 64) for j in (first, second)]
    gains = jnp.pad(norm_gains, ((0, 2), (0, 384 - ROWS)))
    pack_a = jnp.concatenate(
        [jnp.concatenate([q_cols] + k_cols + v_cols, axis=1), gains], axis=0
    )
    pack_b = pad_rows(
        jnp.concatenate(
            [columns(w, FSL * index, FSL) for w in (gate_weight, up_weight, down_weight)], axis=1
        )
    )
    pack_c = pad_rows(jnp.pad(out_weight, ((0, 0), (0, 64))))

    x_own = widen_features(hidden_in)
    g_own = widen_features(out_grad)
    w_a = gather_yz(pack_a)
    x_all = gather_ctx(x_own).reshape(LEN, WIDE)
    w_b = gather_yz(pack_b)
    w_c = gather_zy(pack_c)
    g_all = gather_ctx(g_own).reshape(LEN, WIDE)

    gain_rows = w_a.reshape(DP, PADDED, 384)[:, ROWS : ROWS + 2, :PADDED].astype(F32)
    gain_rows = jnp.where(jnp.arange(PADDED) < ROWS, gain_rows, 0.0)
    gain_first = gain_rows[:, 0, :].reshape(1, WIDE)
    gain_second = gain_rows[:, 1, :].reshape(1, WIDE)
    cos, sin = rotary_tables()

    h1, qkv, attn, lse = attend(x_all, w_a, gain_first, cos, sin)
    attn_all = gather_ctx(attn)
    attn_wide = jnp.swapaxes(attn_all, 0, 1).reshape(LEN, WIDE)
    x_wide = x_all.astype(F32)
    middle = x_wide + dot(attn_wide, w_c, NT)
    scale_two = lax.rsqrt(jnp.sum(middle * middle, axis=1, keepdims=True) * (1.0 / D) + EPS)
    normed_two = middle * scale_two
    h2 = (normed_two * gain_second).astype(BF)
    gate_up = dot(h2, w_b[:, : 2 * FSL], NN)
    gate, up = gate_up[:, :FSL], gate_up[:, FSL:]
    d_hid = dot(g_all, w_b[:, 2 * FSL :], NN)
    sigma = jax.nn.sigmoid(gate)
    hidden = (gate * sigma * up).astype(BF)
    d_gate = (d_hid * up * sigma * (1.0 + gate * (1.0 - sigma))).astype(BF)
    d_up = (d_hid * gate * sigma).astype(BF)
    d_gu = jnp.concatenate([d_gate, d_up], axis=1)
    d_h2 = dot(d_gu, w_b[:, : 2 * FSL], NT)
    gain_two_part = jnp.sum(d_h2 * normed_two, axis=0)
    d_h2_own = scatter_ctx(d_h2.astype(BF).reshape(CTX, TOK, WIDE))

    def own(v):
        return lax.dynamic_slice_in_dim(v, TOK * index, TOK, 0)

    middle_own, scale_own = own(middle), own(scale_two)
    normed_own = middle_own * scale_own
    e2 = d_h2_own * gain_second
    inner = jnp.sum(e2 * normed_own, axis=1, keepdims=True) * (1.0 / D)
    d_mid = g_own.astype(F32) + scale_own * (e2 - normed_own * inner)
    d_mid_all = gather_ctx(d_mid.astype(BF)).reshape(LEN, WIDE)

    out_part = dot(hidden, w_b[:, 2 * FSL :], NT)
    out_own = middle_own + scatter_ctx(out_part.astype(BF).reshape(CTX, TOK, WIDE))
    hidden_out = narrow_features(out_own.astype(BF))

    ff_terms = jnp.concatenate([dot(h2, d_gu, TN), dot(g_all, hidden, TN)], axis=1)
    ff_own = scatter_dp(ff_terms)

    w_out_cols = columns(w_c, 128 * index, 128)
    d_attn = dot(d_mid_all, w_out_cols, NN).astype(BF)
    d_qkv = attend_back(qkv, attn, lse, d_attn, cos, sin)
    d_h1 = dot(d_qkv, w_a, NT)
    scale_one = lax.rsqrt(jnp.sum(x_wide * x_wide, axis=1, keepdims=True) * (1.0 / D) + EPS)
    gain_one_part = jnp.sum(d_h1 * (x_wide * scale_one), axis=0)
    at_terms = jnp.concatenate([dot(h1, d_qkv, TN), dot(d_mid_all, attn, TN)], axis=1)
    at_terms = at_terms.reshape(DP, PADDED, 512)
    gain_parts = jnp.stack([gain_one_part.reshape(DP, PADDED), gain_two_part.reshape(DP, PADDED)], 1)
    at_terms = lax.dynamic_update_slice(at_terms, gain_parts, (0, ROWS, 0))
    at_own = scatter_dp(at_terms.reshape(WIDE, 512))

    ff_all = gather_ctx(ff_own.astype(BF))
    at_all = gather_ctx(at_own.astype(BF))

    d_h1_own = scatter_ctx(d_h1.astype(BF).reshape(CTX, TOK, WIDE))
    x_f = x_own.astype(F32)
    s_own = lax.rsqrt(jnp.sum(x_f * x_f, axis=1, keepdims=True) * (1.0 / D) + EPS)
    n_own = x_f * s_own
    e1 = d_h1_own * gain_first
    inner = jnp.sum(e1 * n_own, axis=1, keepdims=True) * (1.0 / D)
    in_grad = narrow_features(d_mid + s_own * (e1 - n_own * inner))

    at_wide = at_all.astype(F32)
    gains_grad = jnp.sum(at_wide[:, ROWS : ROWS + 2, :ROWS], axis=0)

    def spread(v, start, width):
        part = v[:, :ROWS, start : start + width]
        return jnp.swapaxes(part, 0, 1).reshape(ROWS, CTX * width)

    def grouped(v):
        return jnp.sum(v[:, :D].reshape(ROWS, KV_HEADS, 3, HEAD_DIM), axis=2).reshape(
            ROWS, KV_HEADS * HEAD_DIM
        )

    q_grad = spread(at_wide, 0, 128)[:, :D]
    k_grad = grouped(spread(at_wide, 128, 128))
    v_grad = grouped(spread(at_wide, 256, 128))
    out_w_grad = spread(at_wide, 384, 128)[:, :D]
    ff_wide = ff_all.astype(F32)
    return (
        hidden_out,
        in_grad,
        gains_grad,
        q_grad,
        k_grad,
        v_grad,
        out_w_grad,
        spread(ff_wide, 0, FSL),
        spread(ff_wide, FSL, FSL),
        spread(ff_wide, 2 * FSL, FSL),
    )


def solution(mesh):
    tokens = P(("dp", "ctx"), None)
    rows = P("dp", None)
    gains = P(None, "dp")
    return jax.shard_map(
        on_device,
        mesh=mesh,
        in_specs=(tokens, tokens, gains) + (rows,) * 7,
        out_specs=(tokens, tokens, gains) + (rows,) * 7,
        check_vma=False,
    )
```

```python
import math

import jax
import jax.numpy as jnp
from jax import lax
from jax.experimental import pallas as pl
from jax.experimental.pallas import tpu as pltpu
from jax.sharding import PartitionSpec as P

D = 960
HEADS = 15
KV_HEADS = 5
HEAD_DIM = 64
FF = 2560
EPS = 1e-05
ROPE_BASE = 100000.0
NEG_FILL = -1e30

ROWS = 60
PADDED = 64
DP = 16
SIDE = 4
CTX = 8
CHIPS = 4
TOK = 128
LEN = 1024
WIDE = DP * PADDED
FSL = FF // CTX
QB = 256

BF = jnp.bfloat16
F32 = jnp.float32
NT = (((1,), (1,)), ((), ()))
TN = (((0,), (0,)), ((), ()))
NN = (((1,), (0,)), ((), ()))


def dot(a, b, dims):
    return lax.dot_general(a, b, dims, preferred_element_type=F32)

NTOK = LEN // QB


def along_x(v, d):
    return lax.ppermute(v, "ctx", [(i, (i + 2 * d) % CTX) for i in range(CTX)])


def other_core(v):
    return lax.ppermute(v, "ctx", [(i, i ^ 1) for i in range(CTX)])


def along_y(v, d):
    return lax.ppermute(
        v, "dp", [(i, (i // SIDE) * SIDE + (i + d) % SIDE) for i in range(DP)]
    )


def along_z(v, d):
    return lax.ppermute(v, "dp", [(i, (i + SIDE * d) % DP) for i in range(DP)])


def placed(pieces, first, count):
    out = jnp.zeros((count,) + pieces[0].shape, pieces[0].dtype)
    for d, piece in enumerate(pieces):
        out = lax.dynamic_update_slice_in_dim(out, piece[None], (first - d) % count, 0)
    return out


def gather_ctx(v):
    mine = [v] + [along_x(v, d) for d in (1, 2, 3)]
    return mine + [other_core(piece) for piece in mine]


def gather_zy(v):
    z = lax.axis_index("dp") // SIDE
    col = placed([v] + [along_z(v, d) for d in (1, 2, 3)], z, SIDE)
    return [col] + [along_y(col, d) for d in (1, 2, 3)]


def gather_dp(copies):
    return lax.all_to_all(copies, "dp", 0, 0, tiled=True).reshape(WIDE, copies.shape[2])


def scatter_dp(terms):
    got = lax.all_to_all(terms, "dp", 0, 0, tiled=True)
    return jnp.sum(got.astype(F32), axis=0).astype(BF)


def call(kernel, out_shape, scratch, flops, name, *args):
    return pl.pallas_call(
        kernel,
        out_shape=out_shape,
        scratch_shapes=scratch,
        cost_estimate=pl.CostEstimate(flops=flops, bytes_accessed=4 << 20, transcendentals=1 << 20),
        name=name,
    )(*args)


def shape(*dims, dtype=BF):
    return jax.ShapeDtypeStruct(dims, dtype)


def place():
    index = lax.axis_index("ctx")
    return lax.div(index, 2), lax.rem(index, 2)


def back(position, d):
    return lax.rem(position - d + SIDE, SIDE)


def piece_index(chip, core, n):
    side = core if n < CHIPS else 1 - core
    return 2 * back(chip, n % CHIPS) + side


def place_tokens(pieces, out_ref):
    chip, core = place()
    for n, piece in enumerate(pieces):
        start = pl.multiple_of(TOK * piece_index(chip, core, n), TOK)
        out_ref[pl.ds(start, TOK), :] = piece[...]


def split_tokens(block_ref, i, keep_ref, give_ref):
    chip, core = place()
    d = lax.rem(i - chip + CHIPS, CHIPS)
    keep_ref[d] = block_ref[pl.ds(pl.multiple_of(TOK * core, TOK), TOK), :]
    give_ref[d] = block_ref[pl.ds(pl.multiple_of(TOK * (1 - core), TOK), TOK), :]


def widen(v):
    zero = jnp.zeros((v.shape[0], PADDED - ROWS), v.dtype)
    parts = []
    for b in range(DP):
        parts += [v[:, ROWS * b : ROWS * (b + 1)], zero]
    return jnp.concatenate(parts, axis=1)


def narrow(v):
    return jnp.concatenate([v[:, PADDED * b : PADDED * b + ROWS] for b in range(DP)], axis=1)


def turned(v):
    lane = lax.broadcasted_iota(jnp.int32, v.shape, 1)
    ahead = pltpu.roll(v, 96, 1)
    behind = pltpu.roll(v, 32, 1)
    return jnp.where(lane % 64 < 32, ahead, behind)


def head_mask(shape, head):
    lane = lax.broadcasted_iota(jnp.int32, shape, 1)
    return (lane // 64) == head


def chosen(index, options):
    out = options[0]
    for j in range(1, len(options)):
        out = jnp.where(index == j, options[j], out)
    return out


def pack_kernel(
    x_ref, g_ref, gains_ref, q_ref, k_ref, v_ref, o_ref, gate_ref, up_ref, down_ref,
    xw_ref, gw_ref, a_ref, b_ref, c_ref,
):
    index = lax.axis_index("ctx")
    xw_ref[...] = widen(x_ref[...].astype(F32)).astype(BF)
    gw_ref[...] = widen(g_ref[...].astype(F32)).astype(BF)
    first = lax.div(2 * index, 3)
    second = jnp.minimum(lax.div(2 * index + 1, 3), KV_HEADS - 1)

    def heads(ref):
        w = ref[...].astype(F32)
        slots = [w[:, 64 * j : 64 * (j + 1)] for j in range(KV_HEADS)]
        return [chosen(first, slots), chosen(second, slots)]

    zero = jnp.zeros((ROWS, 64), F32)
    q = jnp.concatenate([q_ref[...].astype(F32), zero], axis=1)
    q_cols = chosen(index, [q[:, 128 * j : 128 * (j + 1)] for j in range(CTX)])
    top = jnp.concatenate([q_cols] + heads(k_ref) + heads(v_ref), axis=1)
    gains = jnp.concatenate([gains_ref[...].astype(F32), jnp.zeros((2, 384 - ROWS), F32)], axis=1)
    low = jnp.concatenate([gains, jnp.zeros((2, 384), F32)], axis=0)
    a = jnp.concatenate([top, low], axis=0).astype(BF)
    cols = []
    for ref in (gate_ref, up_ref, down_ref):
        w = ref[...].astype(F32)
        cols.append(chosen(index, [w[:, FSL * j : FSL * (j + 1)] for j in range(CTX)]))
    b = jnp.concatenate(
        [jnp.concatenate(cols, axis=1), jnp.zeros((PADDED - ROWS, 3 * FSL), F32)], axis=0
    ).astype(BF)
    for n in range(DP):
        a_ref[n] = a
        b_ref[n] = b
    o = jnp.concatenate([o_ref[...].astype(F32), zero], axis=1)
    c_ref[...] = jnp.concatenate([o, jnp.zeros((PADDED - ROWS, WIDE), F32)], axis=0).astype(BF)


def forward_kernel(
    x0, x1, x2, x3, x4, x5, x6, x7, w_ref, cos_ref, sin_ref,
    x_ref, h_ref, qkv_ref, attn_ref, lse_ref, gain_ref, vt_ref,
):
    place_tokens((x0, x1, x2, x3, x4, x5, x6, x7), x_ref)
    gains = jnp.concatenate(
        [w_ref[PADDED * b : PADDED * (b + 1), 0:PADDED].astype(F32)[ROWS : ROWS + 2] for b in range(DP)],
        axis=1,
    )
    gain_ref[0:2, :] = gains
    gain = gains[0:1]
    for i in range(NTOK):
        rows = pl.ds(i * QB, QB)
        x = x_ref[rows, :].astype(F32)
        scale = lax.rsqrt(jnp.sum(x * x, axis=1, keepdims=True) * (1.0 / D) + EPS)
        h = (x * scale * gain).astype(BF)
        h_ref[rows, :] = h
        qkv = dot(h, w_ref[...], NN)
        cos, sin = cos_ref[rows, :], sin_ref[rows, :]
        q, k = qkv[:, :128], qkv[:, 128:256]
        qkv_ref[rows, 0:128] = (q * cos + turned(q) * sin).astype(BF)
        qkv_ref[rows, 128:256] = (k * cos + turned(k) * sin).astype(BF)
        v = qkv[:, 256:384].astype(BF)
        qkv_ref[rows, 256:384] = v
        vt_ref[:, i * QB : (i + 1) * QB] = v.T
    for i in range(NTOK):
        span = (i + 1) * QB
        q = qkv_ref[pl.ds(i * QB, QB), 0:128]
        keys = qkv_ref[pl.ds(0, span), 128:256]
        halves = []
        for head in range(2):
            qm = jnp.where(head_mask(q.shape, head), q, jnp.zeros_like(q)) * BF(0.125)
            s = dot(keys, qm, NT)
            kpos = lax.broadcasted_iota(jnp.int32, s.shape, 0)
            qpos = lax.broadcasted_iota(jnp.int32, s.shape, 1) + i * QB
            s = jnp.where(kpos <= qpos, s, NEG_FILL)
            peak = jnp.max(s, axis=0, keepdims=True)
            p = jnp.exp(s - peak)
            total = jnp.sum(p, axis=0, keepdims=True)
            o = dot(vt_ref[64 * head : 64 * head + 64, 0:span], p.astype(BF), NN)
            halves.append(o / total)
            lse_ref[head : head + 1, i * QB : (i + 1) * QB] = peak + jnp.log(total)
        attn_ref[pl.ds(i * QB, QB), :] = jnp.concatenate(halves, axis=0).T.astype(BF)


def branch_kernel(
    a0, a1, a2, a3, a4, a5, a6, a7, c0, c1, c2, c3, g0, g1, g2, g3, g4, g5, g6, g7,
    x_ref, w_ref, gain_ref,
    keep_ref, give_ref, mid_ref, h_ref, dg_ref, du_ref, hid_ref, g_ref, wo_ref, part_ref,
    attn_ref, wide_ref, wg_ref, wu_ref, wd_ref, all_mid_ref, block_ref,
):
    chip, core = place()
    index = 2 * chip + core
    y = lax.rem(lax.axis_index("dp"), SIDE)
    for n, piece in enumerate((a0, a1, a2, a3, a4, a5, a6, a7)):
        start = pl.multiple_of(128 * piece_index(chip, core, n), 128)
        attn_ref[:, pl.ds(start, 128)] = piece[...]
    for d, piece in enumerate((c0, c1, c2, c3)):
        for z in range(SIDE):
            start = pl.multiple_of(PADDED * (SIDE * z + back(y, d)), PADDED)
            wide_ref[pl.ds(start, PADDED), :] = piece[z]
    place_tokens((g0, g1, g2, g3, g4, g5, g6, g7), g_ref)
    wo_ref[...] = wide_ref[:, pl.ds(pl.multiple_of(128 * index, 128), 128)]
    wg_ref[...] = w_ref[:, 0:FSL]
    wu_ref[...] = w_ref[:, FSL : 2 * FSL]
    wd_ref[...] = w_ref[:, 2 * FSL : 3 * FSL]
    gain = gain_ref[1:2, :]
    part_ref[...] = jnp.zeros_like(part_ref)

    def step(i, carry):
        rows = pl.ds(pl.multiple_of(i * QB, QB), QB)
        mid = x_ref[rows, :].astype(F32) + dot(attn_ref[rows, :], wide_ref[...], NT)
        all_mid_ref[rows, :] = mid
        scale = lax.rsqrt(jnp.sum(mid * mid, axis=1, keepdims=True) * (1.0 / D) + EPS)
        normed = mid * scale
        h = (normed * gain).astype(BF)
        h_ref[rows, :] = h
        gate = dot(h, wg_ref[...], NN)
        up = dot(h, wu_ref[...], NN)
        d_hid = dot(g_ref[rows, :], wd_ref[...], NN)
        sigma = 1.0 / (1.0 + jnp.exp(-gate))
        swish = gate * sigma
        hid_ref[rows, :] = (swish * up).astype(BF)
        dg = (d_hid * up * sigma * (1.0 + gate * (1.0 - sigma))).astype(BF)
        du = (d_hid * swish).astype(BF)
        dg_ref[rows, :] = dg
        du_ref[rows, :] = du
        dh = dot(dg, wg_ref[...], NT) + dot(du, wu_ref[...], NT)
        part_ref[0:1, :] += jnp.sum(dh * normed, axis=0, keepdims=True)
        block_ref[...] = dh.astype(BF)
        split_tokens(block_ref, i, keep_ref, give_ref)
        return carry

    lax.fori_loop(0, NTOK, step, 0)
    mid_ref[...] = all_mid_ref[pl.ds(pl.multiple_of(TOK * index, TOK), TOK), :]


def terms_kernel(
    h_ref, g_ref, dg_ref, du_ref, hid_ref, w_ref, keep_ref, give_ref, out_ref,
    t_ref, wd_ref, block_ref,
):
    wd_ref[...] = w_ref[:, 2 * FSL : 3 * FSL]

    def step(i, carry):
        rows = pl.ds(pl.multiple_of(i * QB, QB), QB)
        hid = hid_ref[rows, :]
        block_ref[...] = dot(hid, wd_ref[...], NT).astype(BF)
        split_tokens(block_ref, i, keep_ref, give_ref)
        t_ref[0:FSL, rows] = dg_ref[rows, :].T
        t_ref[FSL : 2 * FSL, rows] = du_ref[rows, :].T
        t_ref[2 * FSL : 3 * FSL, rows] = hid.T
        return carry

    lax.fori_loop(0, NTOK, step, 0)
    for i in range(NTOK):
        cols = slice(i * QB, (i + 1) * QB)
        gu = dot(t_ref[0 : 2 * FSL, :], h_ref[:, cols], NN)
        dn = dot(t_ref[2 * FSL : 3 * FSL, :], g_ref[:, cols], NN)
        both = jnp.concatenate([gu, dn], axis=0).T.astype(BF)
        for b in range(QB // PADDED):
            out_ref[i * (QB // PADDED) + b] = both[PADDED * b : PADDED * (b + 1), :]


def pair_kernel(keep_ref, got_ref, p0_ref, p1_ref, p2_ref, p3_ref):
    for d, ref in enumerate((p0_ref, p1_ref, p2_ref, p3_ref)):
        ref[...] = (keep_ref[d].astype(F32) + got_ref[d].astype(F32)).astype(ref.dtype)


def summed(p0, p1, p2, p3):
    return p0[...] + p1[...].astype(F32) + p2[...].astype(F32) + p3[...].astype(F32)


def middle_kernel(p0, p1, p2, p3, mid_ref, g_ref, gain_ref, dm_ref, low_ref):
    mid = mid_ref[...]
    scale = lax.rsqrt(jnp.sum(mid * mid, axis=1, keepdims=True) * (1.0 / D) + EPS)
    normed = mid * scale
    e = summed(p0, p1, p2, p3) * gain_ref[1:2, :]
    inner = jnp.sum(e * normed, axis=1, keepdims=True) * (1.0 / D)
    dm = g_ref[...].astype(F32) + scale * (e - normed * inner)
    dm_ref[...] = dm
    low_ref[...] = dm.astype(BF)


def hidden_kernel(p0, p1, p2, p3, mid_ref, out_ref):
    out_ref[...] = narrow(mid_ref[...] + summed(p0, p1, p2, p3)).astype(BF)


def input_kernel(p0, p1, p2, p3, x_ref, dm_ref, gain_ref, out_ref):
    x = x_ref[...].astype(F32)
    scale = lax.rsqrt(jnp.sum(x * x, axis=1, keepdims=True) * (1.0 / D) + EPS)
    normed = x * scale
    e = summed(p0, p1, p2, p3) * gain_ref[0:1, :]
    inner = jnp.sum(e * normed, axis=1, keepdims=True) * (1.0 / D)
    out_ref[...] = narrow(dm_ref[...] + scale * (e - normed * inner))


def backward_kernel(
    m0, m1, m2, m3, m4, m5, m6, m7,
    qkv_ref, attn_ref, lse_ref, wo_ref, x_ref, h_ref, w_ref, gain_ref, part_ref, cos_ref, sin_ref,
    keep_ref, give_ref, out_ref,
    dm_ref, kt_ref, dk_ref, dv_ref, dqkv_ref, t_ref, block_ref, ones_ref,
):
    place_tokens((m0, m1, m2, m3, m4, m5, m6, m7), dm_ref)
    dk_ref[...] = jnp.zeros_like(dk_ref)
    dv_ref[...] = jnp.zeros_like(dv_ref)
    kt_ref[...] = qkv_ref[:, 128:256].T
    for i in range(NTOK):
        rows = pl.ds(i * QB, QB)
        span = (i + 1) * QB
        q = qkv_ref[rows, 0:128]
        keys = qkv_ref[pl.ds(0, span), 128:256]
        values = qkv_ref[pl.ds(0, span), 256:384]
        g = dot(dm_ref[rows, :], wo_ref[...], NN).astype(BF)
        attn = attn_ref[rows, :]
        t_ref[384:512, i * QB : (i + 1) * QB] = attn.T
        prod = (g.astype(F32) * attn.astype(F32)).T
        halves = []
        for head in range(2):
            mask = head_mask(q.shape, head)
            qm = jnp.where(mask, q, jnp.zeros_like(q))
            gm = jnp.where(mask, g, jnp.zeros_like(g))
            delta = jnp.sum(prod[64 * head : 64 * head + 64, :], axis=0, keepdims=True)
            s = dot(keys, qm * BF(0.125), NT) - lse_ref[head : head + 1, i * QB : (i + 1) * QB]
            kpos = lax.broadcasted_iota(jnp.int32, s.shape, 0)
            qpos = lax.broadcasted_iota(jnp.int32, s.shape, 1) + i * QB
            p = jnp.exp(jnp.where(kpos <= qpos, s, NEG_FILL))
            dv_ref[pl.ds(0, span), :] += dot(p.astype(BF), gm, NN)
            dp = dot(values, gm, NT)
            ds = (p * (dp - delta) * 0.125).astype(BF)
            dk_ref[pl.ds(0, span), :] += dot(ds, qm, NN)
            halves.append(dot(kt_ref[64 * head : 64 * head + 64, 0:span], ds, NN))
        dq = jnp.concatenate(halves, axis=0).T
        dqkv_ref[rows, 0:128] = (dq * cos_ref[rows, :] - turned(dq) * sin_ref[rows, :]).astype(BF)
    dk = dk_ref[...]
    dqkv_ref[:, 128:256] = (dk * cos_ref[...] - turned(dk) * sin_ref[...]).astype(BF)
    dqkv_ref[:, 256:384] = dv_ref[...].astype(BF)
    ones_ref[...] = jnp.zeros_like(ones_ref)

    def step(i, carry):
        rows = pl.ds(pl.multiple_of(i * QB, QB), QB)
        dqkv = dqkv_ref[rows, :]
        t_ref[0:384, rows] = dqkv.T
        dh = dot(dqkv, w_ref[...], NT)
        x = x_ref[rows, :].astype(F32)
        scale = lax.rsqrt(jnp.sum(x * x, axis=1, keepdims=True) * (1.0 / D) + EPS)
        ones_ref[0:1, :] += jnp.sum(dh * (x * scale), axis=0, keepdims=True)
        block_ref[...] = dh.astype(BF)
        split_tokens(block_ref, i, keep_ref, give_ref)
        return carry

    lax.fori_loop(0, NTOK, step, 0)
    for i in range(NTOK):
        cols = slice(i * QB, (i + 1) * QB)
        qkv_t = dot(t_ref[0:384, :], h_ref[:, cols], NN)
        o_t = dot(t_ref[384:512, :], dm_ref[:, cols], NN)
        both = jnp.concatenate([qkv_t, o_t], axis=0).T
        for b in range(QB // PADDED):
            block = i * (QB // PADDED) + b
            lanes = slice(PADDED * block, PADDED * (block + 1))
            low = jnp.concatenate([ones_ref[0:1, lanes], part_ref[0:1, lanes]], axis=0)
            low = jnp.concatenate([low, jnp.zeros((2, 512 - PADDED), F32)], axis=1)
            low = jnp.concatenate([low, jnp.zeros((2, 512), F32)], axis=0)
            top = both[PADDED * b : PADDED * b + ROWS, :]
            out_ref[block] = jnp.concatenate([top, low], axis=0).astype(BF)


def place_blocks(pieces, buf_ref):
    chip, core = place()
    for n, piece in enumerate(pieces):
        buf_ref[piece_index(chip, core, n)] = piece[...].astype(F32)


def ff_grads_kernel(p0, p1, p2, p3, p4, p5, p6, p7, gate_ref, up_ref, down_ref, buf_ref):
    place_blocks((p0, p1, p2, p3, p4, p5, p6, p7), buf_ref)
    for n, ref in enumerate((gate_ref, up_ref, down_ref)):
        ref[...] = jnp.concatenate(
            [buf_ref[j, 0:ROWS, FSL * n : FSL * (n + 1)] for j in range(CTX)], axis=1
        )


def attn_grads_kernel(
    p0, p1, p2, p3, p4, p5, p6, p7, gains_ref, q_ref, k_ref, v_ref, o_ref, buf_ref
):
    place_blocks((p0, p1, p2, p3, p4, p5, p6, p7), buf_ref)
    total = buf_ref[0, ROWS : ROWS + 2, 0:ROWS]
    for j in range(1, CTX):
        total = total + buf_ref[j, ROWS : ROWS + 2, 0:ROWS]
    gains_ref[...] = total
    for ref, start in ((q_ref, 0), (o_ref, 384)):
        ref[...] = jnp.concatenate(
            [buf_ref[j, 0:ROWS, start : start + 128] for j in range(CTX)], axis=1
        )[:, :D]
    for ref, start in ((k_ref, 128), (v_ref, 256)):
        slots = []
        for n in range(HEADS):
            at = start + 64 * (n % 2)
            slots.append(buf_ref[n // 2, 0:ROWS, at : at + 64])
        ref[...] = jnp.concatenate(
            [slots[3 * j] + slots[3 * j + 1] + slots[3 * j + 2] for j in range(KV_HEADS)], axis=1
        )


def rotary_tables():
    half = HEAD_DIM // 2
    freq = ROPE_BASE ** (-(jnp.arange(half, dtype=F32) * 2.0) / HEAD_DIM)
    angles = jnp.arange(LEN, dtype=F32)[:, None] * freq[None, :]
    c, s = jnp.cos(angles), jnp.sin(angles)
    return jnp.concatenate([c, c, c, c], axis=1), jnp.concatenate([-s, s, -s, s], axis=1)


def reduce_ctx(keep, give):
    one = shape(TOK, WIDE)
    p0, p1, p2, p3 = call(
        pair_kernel, (shape(TOK, WIDE, dtype=F32), one, one, one), [], 1 << 20, "pair", keep, other_core(give)
    )
    return [p0] + [along_x(p, d) for d, p in ((1, p1), (2, p2), (3, p3))]


def on_device(
    hidden_in,
    out_grad,
    norm_gains,
    q_weight,
    k_weight,
    v_weight,
    out_weight,
    gate_weight,
    up_weight,
    down_weight,
):
    gf = 1 << 30
    x_own, g_own, pack_a, pack_b, pack_c = call(
        pack_kernel,
        (shape(TOK, WIDE), shape(TOK, WIDE), shape(DP, PADDED, 384), shape(DP, PADDED, 3 * FSL), shape(PADDED, WIDE)),
        [],
        1 << 20,
        "pack",
        hidden_in, out_grad, norm_gains, q_weight, k_weight, v_weight, out_weight,
        gate_weight, up_weight, down_weight,
    )
    cos, sin = rotary_tables()
    w_a = gather_dp(pack_a)
    x_pieces = gather_ctx(x_own)
    w_a, x_pieces, pack_b, pack_c, g_own = lax.optimization_barrier(
        (w_a, x_pieces, pack_b, pack_c, g_own)
    )
    w_b = gather_dp(pack_b)
    c_pieces = gather_zy(pack_c)
    g_pieces = gather_ctx(g_own)

    tall, narrow_bf = shape(LEN, WIDE), shape(LEN, FSL)
    split = shape(CHIPS, TOK, WIDE)
    x_all, h1, qkv, attn, lse, gains = call(
        forward_kernel,
        (tall, tall, shape(LEN, 384), shape(LEN, 128), shape(8, LEN, dtype=F32), shape(8, WIDE, dtype=F32)),
        [pltpu.VMEM((128, LEN), BF)],
        2 * gf,
        "attend_forward",
        *x_pieces, w_a, cos, sin,
    )
    attn_pieces = gather_ctx(attn)
    keep, give, mid_own, h2, d_gate, d_up, hidden, g_all, wo_own, gain_two = call(
        branch_kernel,
        (split, split, shape(TOK, WIDE, dtype=F32), tall, narrow_bf, narrow_bf, narrow_bf, tall,
         shape(LEN, 128), shape(8, WIDE, dtype=F32)),
        [
            pltpu.VMEM((LEN, WIDE), BF),
            pltpu.VMEM((WIDE, WIDE), BF),
            pltpu.VMEM((WIDE, FSL), BF),
            pltpu.VMEM((WIDE, FSL), BF),
            pltpu.VMEM((WIDE, FSL), BF),
            pltpu.VMEM((LEN, WIDE), F32),
            pltpu.VMEM((QB, WIDE), BF),
        ],
        6 * gf,
        "branch",
        *attn_pieces, *c_pieces, *g_pieces, x_all, w_b, gains,
    )
    dh2_parts = reduce_ctx(keep, give)
    d_mid, d_mid_low = call(
        middle_kernel,
        (shape(TOK, WIDE, dtype=F32), shape(TOK, WIDE)),
        [],
        1 << 20,
        "middle",
        *dh2_parts, mid_own, g_own, gains,
    )
    m_pieces = gather_ctx(d_mid_low)
    keep_out, give_out, ff_terms = call(
        terms_kernel,
        (split, split, shape(DP, PADDED, 3 * FSL)),
        [pltpu.VMEM((3 * FSL, LEN), BF), pltpu.VMEM((WIDE, FSL), BF), pltpu.VMEM((QB, WIDE), BF)],
        3 * gf,
        "terms",
        h2, g_all, d_gate, d_up, hidden, w_b,
    )
    ff_own = scatter_dp(ff_terms)
    keep_in, give_in, at_terms = call(
        backward_kernel,
        (split, split, shape(DP, PADDED, 512)),
        [
            pltpu.VMEM((LEN, WIDE), BF),
            pltpu.VMEM((128, LEN), BF),
            pltpu.VMEM((LEN, 128), F32),
            pltpu.VMEM((LEN, 128), F32),
            pltpu.VMEM((LEN, 384), BF),
            pltpu.VMEM((512, LEN), BF),
            pltpu.VMEM((QB, WIDE), BF),
            pltpu.VMEM((8, WIDE), F32),
        ],
        4 * gf,
        "attend_backward",
        *m_pieces, qkv, attn, lse, wo_own, x_all, h1, w_a, gains, gain_two, cos, sin,
    )
    at_own = scatter_dp(at_terms)
    out_parts = reduce_ctx(keep_out, give_out)
    hidden_out = call(hidden_kernel, shape(TOK, D), [], 1 << 20, "hidden", *out_parts, mid_own)
    ff_pieces = gather_ctx(ff_own)
    ff_grad = shape(ROWS, FF, dtype=F32)
    gate_grad, up_grad, down_grad = call(
        ff_grads_kernel, (ff_grad,) * 3, [pltpu.VMEM((CTX, PADDED, 3 * FSL), F32)], 1 << 20, "ff_grads", *ff_pieces
    )
    dh1_parts = reduce_ctx(keep_in, give_in)
    in_grad = call(
        input_kernel, shape(TOK, D, dtype=F32), [], 1 << 20, "input_grad", *dh1_parts, x_own, d_mid, gains
    )
    at_pieces = gather_ctx(at_own)
    gains_grad, q_grad, k_grad, v_grad, o_grad = call(
        attn_grads_kernel,
        (shape(2, ROWS, dtype=F32), shape(ROWS, D, dtype=F32), shape(ROWS, 320, dtype=F32),
         shape(ROWS, 320, dtype=F32), shape(ROWS, D, dtype=F32)),
        [pltpu.VMEM((CTX, PADDED, 512), F32)],
        1 << 20,
        "attn_grads",
        *at_pieces,
    )
    return (
        hidden_out, in_grad, gains_grad, q_grad, k_grad, v_grad, o_grad, gate_grad, up_grad, down_grad
    )


def solution(mesh):
    tokens = P(("dp", "ctx"), None)
    rows = P("dp", None)
    gains = P(None, "dp")
    return jax.shard_map(
        on_device,
        mesh=mesh,
        in_specs=(tokens, tokens, gains) + (rows,) * 7,
        out_specs=(tokens, tokens, gains) + (rows,) * 7,
        check_vma=False,
    )
```

```python
import math

import jax
import jax.numpy as jnp
from jax import lax
from jax.experimental import pallas as pl
from jax.experimental.pallas import tpu as pltpu
from jax.sharding import PartitionSpec as P

D = 960
HEADS = 15
KV_HEADS = 5
HEAD_DIM = 64
FF = 2560
EPS = 1e-05
ROPE_BASE = 100000.0
NEG_FILL = -1e30

ROWS = 60
PADDED = 64
DP = 16
SIDE = 4
CTX = 8
CHIPS = 4
TOK = 128
LEN = 1024
WIDE = DP * PADDED
FSL = FF // CTX
QB = 256

BF = jnp.bfloat16
F32 = jnp.float32
NT = (((1,), (1,)), ((), ()))
TN = (((0,), (0,)), ((), ()))
NN = (((1,), (0,)), ((), ()))


def dot(a, b, dims):
    return lax.dot_general(a, b, dims, preferred_element_type=F32)

NTOK = LEN // QB


def along_x(v, d):
    return lax.ppermute(v, "ctx", [(i, (i + 2 * d) % CTX) for i in range(CTX)])


def other_core(v):
    return lax.ppermute(v, "ctx", [(i, i ^ 1) for i in range(CTX)])


def gather_ctx(v):
    mine = jnp.stack([v] + [along_x(v, d) for d in (1, 2, 3)])
    return mine, other_core(mine)


def gather_small(v):
    both = jnp.stack([v, other_core(v)])
    return [both] + [along_x(both, d) for d in (1, 2, 3)]


together = lax.optimization_barrier


def gather_dp(copies):
    return lax.all_to_all(copies, "dp", 0, 0, tiled=True).reshape(WIDE, copies.shape[2])


def scatter_dp(terms):
    got = lax.all_to_all(terms, "dp", 0, 0, tiled=True)
    return jnp.sum(got.astype(F32), axis=0).astype(BF)


def call(kernel, out_shape, scratch, flops, name, *args, wait=()):
    taken, events = len(args), len(wait)

    def body(*refs):
        kernel(*refs[:taken], *refs[taken + events :])

    return pl.pallas_call(
        body,
        out_shape=out_shape,
        in_specs=[pl.BlockSpec(memory_space=pltpu.VMEM)] * taken
        + [pl.BlockSpec(memory_space=pl.ANY)] * events,
        scratch_shapes=scratch,
        cost_estimate=pl.CostEstimate(flops=flops, bytes_accessed=4 << 20, transcendentals=1 << 20),
        name=name,
    )(*args, *wait)


def shape(*dims, dtype=BF):
    return jax.ShapeDtypeStruct(dims, dtype)


def place():
    index = lax.axis_index("ctx")
    return lax.div(index, 2), lax.rem(index, 2)


def back(position, d):
    return lax.rem(position - d + SIDE, SIDE)


def pieces(mine_ref, theirs_ref):
    chip, core = place()
    for d in range(CHIPS):
        first = 2 * back(chip, d)
        yield first + core, mine_ref.at[d]
        yield first + 1 - core, theirs_ref.at[d]


def place_tokens(mine_ref, theirs_ref, out_ref):
    for n, piece in pieces(mine_ref, theirs_ref):
        out_ref[pl.ds(pl.multiple_of(TOK * n, TOK), TOK), :] = piece[...]


def split_tokens(block_ref, i, keep_ref, give_ref):
    chip, core = place()
    d = lax.rem(i - chip + CHIPS, CHIPS)
    keep_ref[d] = block_ref[pl.ds(pl.multiple_of(TOK * core, TOK), TOK), :]
    give_ref[d] = block_ref[pl.ds(pl.multiple_of(TOK * (1 - core), TOK), TOK), :]


def widen(v):
    zero = jnp.zeros((PADDED - ROWS, v.shape[1]), v.dtype)
    parts = []
    for b in range(DP):
        parts += [v[ROWS * b : ROWS * (b + 1), :], zero]
    return jnp.concatenate(parts, axis=0).T


def narrow(v):
    t = v.T
    return jnp.concatenate([t[PADDED * b : PADDED * b + ROWS, :] for b in range(DP)], axis=0)


def turned(v):
    lane = lax.broadcasted_iota(jnp.int32, v.shape, 1)
    ahead = pltpu.roll(v, 96, 1)
    behind = pltpu.roll(v, 32, 1)
    return jnp.where(lane % 64 < 32, ahead, behind)


def head_mask(shape, head):
    lane = lax.broadcasted_iota(jnp.int32, shape, 1)
    return (lane // 64) == head


def chosen(index, options):
    out = options[0]
    for j in range(1, len(options)):
        out = jnp.where(index == j, options[j], out)
    return out


def tokens_kernel(x_ref, xw_ref):
    xw_ref[...] = widen(x_ref[...].astype(F32)).astype(BF)


def pack_kernel(
    g_ref, gains_ref, q_ref, k_ref, v_ref, o_ref, gate_ref, up_ref, down_ref,
    gw_ref, a_ref, b_ref,
):
    index = lax.axis_index("ctx")
    core = lax.rem(index, 2)
    gw_ref[...] = widen(g_ref[...].astype(F32)).astype(BF)
    first = lax.div(2 * index, 3)
    second = jnp.minimum(lax.div(2 * index + 1, 3), KV_HEADS - 1)

    def heads(ref):
        w = ref[...].astype(F32)
        slots = [w[:, 64 * j : 64 * (j + 1)] for j in range(KV_HEADS)]
        return [chosen(first, slots), chosen(second, slots)]

    zero = jnp.zeros((ROWS, 64), F32)
    q = jnp.concatenate([q_ref[...].astype(F32), zero], axis=1)
    q_cols = chosen(index, [q[:, 128 * j : 128 * (j + 1)] for j in range(CTX)])
    top = jnp.concatenate([q_cols] + heads(k_ref) + heads(v_ref), axis=1)
    gains = jnp.concatenate([gains_ref[...].astype(F32), jnp.zeros((2, 384 - ROWS), F32)], axis=1)
    low = jnp.concatenate([gains, jnp.zeros((2, 384), F32)], axis=0)
    a = jnp.concatenate([top, low], axis=0).astype(BF)
    cols = []
    for ref in (gate_ref, up_ref, down_ref):
        w = ref[...].astype(F32)
        cols.append(chosen(index, [w[:, FSL * j : FSL * (j + 1)] for j in range(CTX)]))
    for n in range(DP):
        a_ref[n] = a
    o = jnp.concatenate([o_ref[...].astype(F32), zero], axis=1)
    half = chosen(core, [o[:, :512], o[:, 512:]])
    low = jnp.zeros((PADDED - ROWS, 512 + 3 * FSL), F32)
    b = jnp.concatenate([jnp.concatenate([half] + cols, axis=1), low], axis=0).astype(BF)
    for n in range(DP):
        b_ref[n] = b


def forward_kernel(
    mine_ref, theirs_ref, w_ref, cos_ref, sin_ref,
    x_ref, h_ref, qkv_ref, attn_ref, lse_ref, gain_ref, vt_ref,
):
    place_tokens(mine_ref, theirs_ref, x_ref)
    gains = jnp.concatenate(
        [w_ref[PADDED * b : PADDED * (b + 1), 0:PADDED].astype(F32)[ROWS : ROWS + 2] for b in range(DP)],
        axis=1,
    )
    gain_ref[0:2, :] = gains
    gain = gains[0:1]
    for i in range(NTOK):
        rows = pl.ds(i * QB, QB)
        x = x_ref[rows, :].astype(F32)
        scale = lax.rsqrt(jnp.sum(x * x, axis=1, keepdims=True) * (1.0 / D) + EPS)
        h = (x * scale * gain).astype(BF)
        h_ref[rows, :] = h
        qkv = dot(h, w_ref[...], NN)
        cos, sin = cos_ref[rows, :], sin_ref[rows, :]
        q, k = qkv[:, :128], qkv[:, 128:256]
        qkv_ref[rows, 0:128] = (q * cos + turned(q) * sin).astype(BF)
        qkv_ref[rows, 128:256] = (k * cos + turned(k) * sin).astype(BF)
        v = qkv[:, 256:384].astype(BF)
        qkv_ref[rows, 256:384] = v
        vt_ref[:, i * QB : (i + 1) * QB] = v.T
    for i in range(NTOK):
        span = (i + 1) * QB
        q = qkv_ref[pl.ds(i * QB, QB), 0:128]
        keys = qkv_ref[pl.ds(0, span), 128:256]
        halves = []
        for head in range(2):
            qm = jnp.where(head_mask(q.shape, head), q, jnp.zeros_like(q)) * BF(0.125)
            s = dot(keys, qm, NT)
            kpos = lax.broadcasted_iota(jnp.int32, s.shape, 0)
            qpos = lax.broadcasted_iota(jnp.int32, s.shape, 1) + i * QB
            s = jnp.where(kpos <= qpos, s, NEG_FILL)
            peak = jnp.max(s, axis=0, keepdims=True)
            p = jnp.exp(s - peak)
            total = jnp.sum(p, axis=0, keepdims=True)
            o = dot(vt_ref[64 * head : 64 * head + 64, 0:span], p.astype(BF), NN)
            halves.append(o / total)
            lse_ref[head : head + 1, i * QB : (i + 1) * QB] = peak + jnp.log(total)
        attn_ref[pl.ds(i * QB, QB), :] = jnp.concatenate(halves, axis=0).T.astype(BF)


def branch_kernel(
    amine_ref, atheirs_ref, w_ref, wother_ref, gmine_ref, gtheirs_ref, x_ref, gain_ref,
    keep_ref, give_ref, mid_ref, h_ref, dg_ref, du_ref, hid_ref, g_ref, wo_ref, part_ref, wd_ref,
    attn_ref, wide_ref, wg_ref, wu_ref, all_mid_ref, block_ref,
):
    chip, core = place()
    index = 2 * chip + core
    for n, piece in pieces(amine_ref, atheirs_ref):
        attn_ref[:, pl.ds(pl.multiple_of(128 * n, 128), 128)] = piece[...]
    wide_ref[:, pl.ds(pl.multiple_of(512 * core, 512), 512)] = w_ref[:, 0:512]
    wide_ref[:, pl.ds(pl.multiple_of(512 * (1 - core), 512), 512)] = wother_ref[...]
    wg_ref[...] = w_ref[:, 512 : 512 + FSL]
    wu_ref[...] = w_ref[:, 512 + FSL : 512 + 2 * FSL]
    wd_ref[...] = w_ref[:, 512 + 2 * FSL : 512 + 3 * FSL]
    place_tokens(gmine_ref, gtheirs_ref, g_ref)
    wo_ref[...] = wide_ref[:, pl.ds(pl.multiple_of(128 * index, 128), 128)]
    gain = gain_ref[1:2, :]
    part_ref[...] = jnp.zeros_like(part_ref)

    def step(i, carry):
        rows = pl.ds(pl.multiple_of(i * QB, QB), QB)
        mid = x_ref[rows, :].astype(F32) + dot(attn_ref[rows, :], wide_ref[...], NT)
        all_mid_ref[rows, :] = mid
        scale = lax.rsqrt(jnp.sum(mid * mid, axis=1, keepdims=True) * (1.0 / D) + EPS)
        normed = mid * scale
        h = (normed * gain).astype(BF)
        h_ref[rows, :] = h
        gate = dot(h, wg_ref[...], NN)
        up = dot(h, wu_ref[...], NN)
        d_hid = dot(g_ref[rows, :], wd_ref[...], NN)
        sigma = 1.0 / (1.0 + jnp.exp(-gate))
        swish = gate * sigma
        hid_ref[rows, :] = (swish * up).astype(BF)
        dg = (d_hid * up * sigma * (1.0 + gate * (1.0 - sigma))).astype(BF)
        du = (d_hid * swish).astype(BF)
        dg_ref[rows, :] = dg
        du_ref[rows, :] = du
        dh = dot(dg, wg_ref[...], NT) + dot(du, wu_ref[...], NT)
        part_ref[0:1, :] += jnp.sum(dh * normed, axis=0, keepdims=True)
        block_ref[...] = dh.astype(BF)
        split_tokens(block_ref, i, keep_ref, give_ref)
        return carry

    lax.fori_loop(0, NTOK, step, 0)
    mid_ref[...] = all_mid_ref[pl.ds(pl.multiple_of(TOK * index, TOK), TOK), :]


def terms_kernel(
    h_ref, g_ref, dg_ref, du_ref, hid_ref, wd_ref, keep_ref, give_ref, out_ref,
    t_ref, block_ref,
):

    def step(i, carry):
        rows = pl.ds(pl.multiple_of(i * QB, QB), QB)
        hid = hid_ref[rows, :]
        block_ref[...] = dot(hid, wd_ref[...], NT).astype(BF)
        split_tokens(block_ref, i, keep_ref, give_ref)
        t_ref[0:FSL, rows] = dg_ref[rows, :].T
        t_ref[FSL : 2 * FSL, rows] = du_ref[rows, :].T
        t_ref[2 * FSL : 3 * FSL, rows] = hid.T
        return carry

    lax.fori_loop(0, NTOK, step, 0)
    for i in range(NTOK):
        cols = slice(i * QB, (i + 1) * QB)
        gu = dot(t_ref[0 : 2 * FSL, :], h_ref[:, cols], NN)
        dn = dot(t_ref[2 * FSL : 3 * FSL, :], g_ref[:, cols], NN)
        both = jnp.concatenate([gu, dn], axis=0).T.astype(BF)
        for b in range(QB // PADDED):
            out_ref[i * (QB // PADDED) + b] = both[PADDED * b : PADDED * (b + 1), :]


def pair_kernel(keep_ref, got_ref, p0_ref, p1_ref, p2_ref, p3_ref):
    for d, ref in enumerate((p0_ref, p1_ref, p2_ref, p3_ref)):
        ref[...] = (keep_ref[d].astype(F32) + got_ref[d].astype(F32)).astype(ref.dtype)


def summed(p0, p1, p2, p3):
    return p0[...] + p1[...].astype(F32) + p2[...].astype(F32) + p3[...].astype(F32)


def middle_kernel(p0, p1, p2, p3, mid_ref, g_ref, gain_ref, dm_ref, low_ref):
    mid = mid_ref[...]
    scale = lax.rsqrt(jnp.sum(mid * mid, axis=1, keepdims=True) * (1.0 / D) + EPS)
    normed = mid * scale
    e = summed(p0, p1, p2, p3) * gain_ref[1:2, :]
    inner = jnp.sum(e * normed, axis=1, keepdims=True) * (1.0 / D)
    dm = g_ref[...].astype(F32) + scale * (e - normed * inner)
    dm_ref[...] = dm
    low_ref[...] = dm.astype(BF)


def hidden_kernel(p0, p1, p2, p3, mid_ref, out_ref):
    out_ref[...] = narrow(mid_ref[...] + summed(p0, p1, p2, p3)).astype(BF)


def input_kernel(p0, p1, p2, p3, x_ref, dm_ref, gain_ref, out_ref):
    x = x_ref[...].astype(F32)
    scale = lax.rsqrt(jnp.sum(x * x, axis=1, keepdims=True) * (1.0 / D) + EPS)
    normed = x * scale
    e = summed(p0, p1, p2, p3) * gain_ref[0:1, :]
    inner = jnp.sum(e * normed, axis=1, keepdims=True) * (1.0 / D)
    out_ref[...] = narrow(dm_ref[...] + scale * (e - normed * inner))


def backward_kernel(
    mine_ref, theirs_ref,
    qkv_ref, attn_ref, lse_ref, wo_ref, x_ref, h_ref, w_ref, gain_ref, part_ref, cos_ref, sin_ref,
    keep_ref, give_ref, out_ref,
    dm_ref, kt_ref, dk_ref, dv_ref, dqkv_ref, t_ref, block_ref, ones_ref,
):
    place_tokens(mine_ref, theirs_ref, dm_ref)
    dk_ref[...] = jnp.zeros_like(dk_ref)
    dv_ref[...] = jnp.zeros_like(dv_ref)
    kt_ref[...] = qkv_ref[:, 128:256].T
    for i in range(NTOK):
        rows = pl.ds(i * QB, QB)
        span = (i + 1) * QB
        q = qkv_ref[rows, 0:128]
        keys = qkv_ref[pl.ds(0, span), 128:256]
        values = qkv_ref[pl.ds(0, span), 256:384]
        g = dot(dm_ref[rows, :], wo_ref[...], NN).astype(BF)
        attn = attn_ref[rows, :]
        t_ref[384:512, i * QB : (i + 1) * QB] = attn.T
        prod = (g.astype(F32) * attn.astype(F32)).T
        halves = []
        for head in range(2):
            mask = head_mask(q.shape, head)
            qm = jnp.where(mask, q, jnp.zeros_like(q))
            gm = jnp.where(mask, g, jnp.zeros_like(g))
            delta = jnp.sum(prod[64 * head : 64 * head + 64, :], axis=0, keepdims=True)
            s = dot(keys, qm * BF(0.125), NT) - lse_ref[head : head + 1, i * QB : (i + 1) * QB]
            kpos = lax.broadcasted_iota(jnp.int32, s.shape, 0)
            qpos = lax.broadcasted_iota(jnp.int32, s.shape, 1) + i * QB
            p = jnp.exp(jnp.where(kpos <= qpos, s, NEG_FILL))
            dv_ref[pl.ds(0, span), :] += dot(p.astype(BF), gm, NN)
            dp = dot(values, gm, NT)
            ds = (p * (dp - delta) * 0.125).astype(BF)
            dk_ref[pl.ds(0, span), :] += dot(ds, qm, NN)
            halves.append(dot(kt_ref[64 * head : 64 * head + 64, 0:span], ds, NN))
        dq = jnp.concatenate(halves, axis=0).T
        dqkv_ref[rows, 0:128] = (dq * cos_ref[rows, :] - turned(dq) * sin_ref[rows, :]).astype(BF)
    dk = dk_ref[...]
    dqkv_ref[:, 128:256] = (dk * cos_ref[...] - turned(dk) * sin_ref[...]).astype(BF)
    dqkv_ref[:, 256:384] = dv_ref[...].astype(BF)
    ones_ref[...] = jnp.zeros_like(ones_ref)

    def step(i, carry):
        rows = pl.ds(pl.multiple_of(i * QB, QB), QB)
        dqkv = dqkv_ref[rows, :]
        t_ref[0:384, rows] = dqkv.T
        dh = dot(dqkv, w_ref[...], NT)
        x = x_ref[rows, :].astype(F32)
        scale = lax.rsqrt(jnp.sum(x * x, axis=1, keepdims=True) * (1.0 / D) + EPS)
        ones_ref[0:1, :] += jnp.sum(dh * (x * scale), axis=0, keepdims=True)
        block_ref[...] = dh.astype(BF)
        split_tokens(block_ref, i, keep_ref, give_ref)
        return carry

    lax.fori_loop(0, NTOK, step, 0)
    for i in range(NTOK):
        cols = slice(i * QB, (i + 1) * QB)
        qkv_t = dot(t_ref[0:384, :], h_ref[:, cols], NN)
        o_t = dot(t_ref[384:512, :], dm_ref[:, cols], NN)
        both = jnp.concatenate([qkv_t, o_t], axis=0).T
        for b in range(QB // PADDED):
            block = i * (QB // PADDED) + b
            lanes = slice(PADDED * block, PADDED * (block + 1))
            low = jnp.concatenate([ones_ref[0:1, lanes], part_ref[0:1, lanes]], axis=0)
            low = jnp.concatenate([low, jnp.zeros((2, 512 - PADDED), F32)], axis=1)
            low = jnp.concatenate([low, jnp.zeros((2, 512), F32)], axis=0)
            top = both[PADDED * b : PADDED * b + ROWS, :]
            out_ref[block] = jnp.concatenate([top, low], axis=0).astype(BF)


def place_blocks(parts, buf_ref):
    chip, core = place()
    for d, piece in enumerate(parts):
        buf_ref[2 * back(chip, d) + core] = piece[0].astype(F32)
        buf_ref[2 * back(chip, d) + 1 - core] = piece[1].astype(F32)


def ff_grads_kernel(p0, p1, p2, p3, gate_ref, up_ref, down_ref, buf_ref):
    place_blocks((p0, p1, p2, p3), buf_ref)
    for n, ref in enumerate((gate_ref, up_ref, down_ref)):
        ref[...] = jnp.concatenate(
            [buf_ref[j, 0:ROWS, FSL * n : FSL * (n + 1)] for j in range(CTX)], axis=1
        )


def attn_grads_kernel(
    p0, p1, p2, p3, gains_ref, q_ref, k_ref, v_ref, o_ref, buf_ref
):
    place_blocks((p0, p1, p2, p3), buf_ref)
    total = buf_ref[0, ROWS : ROWS + 2, 0:ROWS]
    for j in range(1, CTX):
        total = total + buf_ref[j, ROWS : ROWS + 2, 0:ROWS]
    gains_ref[...] = total
    for ref, start in ((q_ref, 0), (o_ref, 384)):
        ref[...] = jnp.concatenate(
            [buf_ref[j, 0:ROWS, start : start + 128] for j in range(CTX)], axis=1
        )[:, :D]
    for ref, start in ((k_ref, 128), (v_ref, 256)):
        slots = []
        for n in range(HEADS):
            at = start + 64 * (n % 2)
            slots.append(buf_ref[n // 2, 0:ROWS, at : at + 64])
        ref[...] = jnp.concatenate(
            [slots[3 * j] + slots[3 * j + 1] + slots[3 * j + 2] for j in range(KV_HEADS)], axis=1
        )


def rotary_tables(positions):
    lane = lax.broadcasted_iota(jnp.int32, (LEN, 128), 1)
    freq = ROPE_BASE ** (-((lane % 32).astype(F32) * 2.0) / HEAD_DIM)
    angles = positions * freq
    return jnp.cos(angles), jnp.where(lane % 64 < 32, -1.0, 1.0) * jnp.sin(angles)


def pair_sum(keep, got):
    one = shape(TOK, WIDE)
    return call(
        pair_kernel, (shape(TOK, WIDE, dtype=F32), one, one, one), [], 1 << 20, "pair", keep, got
    )


def spread_x(pairs):
    return [pairs[0]] + [along_x(pairs[d], d) for d in (1, 2, 3)]


def on_device(
    hidden_in,
    out_grad,
    norm_gains,
    q_weight,
    k_weight,
    v_weight,
    out_weight,
    gate_weight,
    up_weight,
    down_weight,
):
    gf = 1 << 30
    x_own = call(tokens_kernel, shape(TOK, WIDE), [], 1 << 20, "tokens", hidden_in.T)
    x_steps = [along_x(x_own, d) for d in (1, 2, 3)]
    g_own, pack_a, pack_b = call(
        pack_kernel,
        (shape(TOK, WIDE), shape(DP, PADDED, 384), shape(DP, PADDED, 512 + 3 * FSL)),
        [],
        1 << 20,
        "pack",
        out_grad.T, norm_gains, q_weight, k_weight, v_weight, out_weight, gate_weight, up_weight, down_weight,
    )
    w_a = gather_dp(pack_a)
    positions = lax.broadcasted_iota(jnp.int32, (LEN, 128), 0).astype(F32)
    cos, sin = rotary_tables(positions)
    x_steps, cos, sin, g_late = together((x_steps, cos, sin, g_own))
    x_mine = jnp.stack([x_own] + x_steps)
    x_theirs = other_core(x_mine)
    g_steps = [along_x(g_late, d) for d in (1, 2, 3)]
    pack_b, x_mine = together((pack_b, x_mine))
    w_b = gather_dp(pack_b)

    tall, slim = shape(LEN, WIDE), shape(LEN, FSL)
    split = shape(CHIPS, TOK, WIDE)
    x_all, h1, qkv, attn, lse, gains = call(
        forward_kernel,
        (tall, tall, shape(LEN, 384), shape(LEN, 128), shape(8, LEN, dtype=F32), shape(8, WIDE, dtype=F32)),
        [pltpu.VMEM((128, LEN), BF)],
        2 * gf,
        "attend_forward",
        x_mine, x_theirs, w_a, cos, sin,
    )
    g_mine = jnp.stack([g_own] + g_steps)
    g_theirs = other_core(g_mine)
    a_mine, a_theirs = gather_ctx(attn)
    w_other = other_core(w_b[:, :512])
    keep, give, mid_own, h2, d_gate, d_up, hidden, g_all, wo_own, gain_two, w_down = call(
        branch_kernel,
        (split, split, shape(TOK, WIDE, dtype=F32), tall, slim, slim, slim, tall,
         shape(LEN, 128), shape(8, WIDE, dtype=F32), shape(WIDE, FSL)),
        [
            pltpu.VMEM((LEN, WIDE), BF),
            pltpu.VMEM((WIDE, WIDE), BF),
            pltpu.VMEM((WIDE, FSL), BF),
            pltpu.VMEM((WIDE, FSL), BF),
            pltpu.VMEM((LEN, WIDE), F32),
            pltpu.VMEM((QB, WIDE), BF),
        ],
        6 * gf,
        "branch",
        a_mine, a_theirs, w_b, w_other, g_mine, g_theirs, x_all, gains,
    )
    dh2_pairs = pair_sum(keep, other_core(give))
    dh2_parts = spread_x(dh2_pairs)
    keep_out, give_out, ff_terms = call(
        terms_kernel,
        (split, split, shape(DP, PADDED, 3 * FSL)),
        [pltpu.VMEM((3 * FSL, LEN), BF), pltpu.VMEM((QB, WIDE), BF)],
        3 * gf,
        "terms",
        h2, g_all, d_gate, d_up, hidden, w_down,
        wait=(dh2_pairs[1],),
    )
    d_mid, d_mid_low = call(
        middle_kernel,
        (shape(TOK, WIDE, dtype=F32), shape(TOK, WIDE)),
        [],
        1 << 20,
        "middle",
        *dh2_parts, mid_own, g_own, gains,
        wait=(ff_terms,),
    )
    ff_terms, give_out, d_mid_low = together((ff_terms, give_out, d_mid_low))
    m_mine, m_theirs = gather_ctx(d_mid_low)
    ff_own = scatter_dp(ff_terms)
    out_pairs = pair_sum(keep_out, other_core(give_out))
    m_mine, m_theirs, out_pairs = together((m_mine, m_theirs, out_pairs))
    out_parts = spread_x(out_pairs)
    keep_in, give_in, at_terms = call(
        backward_kernel,
        (split, split, shape(DP, PADDED, 512)),
        [
            pltpu.VMEM((LEN, WIDE), BF),
            pltpu.VMEM((128, LEN), BF),
            pltpu.VMEM((LEN, 128), F32),
            pltpu.VMEM((LEN, 128), F32),
            pltpu.VMEM((LEN, 384), BF),
            pltpu.VMEM((512, LEN), BF),
            pltpu.VMEM((QB, WIDE), BF),
            pltpu.VMEM((8, WIDE), F32),
        ],
        4 * gf,
        "attend_backward",
        m_mine, m_theirs, qkv, attn, lse, wo_own, x_all, h1, w_a, gains, gain_two, cos, sin,
    )
    give_in, ff_own, out_parts = together((give_in, ff_own, out_parts))
    dh1_pairs = pair_sum(keep_in, other_core(give_in))
    dh1_pairs, at_terms, ff_own = together((dh1_pairs, at_terms, ff_own))
    dh1_parts = spread_x(dh1_pairs)
    at_own = scatter_dp(at_terms)
    hidden_out = call(
        hidden_kernel, shape(D, TOK), [], 1 << 20, "hidden", *out_parts, mid_own, wait=(dh1_pairs[1],)
    )
    ff_pieces = gather_small(ff_own)
    at_pieces = gather_small(at_own)
    ff_grad = shape(ROWS, FF, dtype=F32)
    gate_grad, up_grad, down_grad = call(
        ff_grads_kernel, (ff_grad,) * 3, [pltpu.VMEM((CTX, PADDED, 3 * FSL), F32)], 1 << 20, "ff_grads", *ff_pieces
    )
    in_grad = call(
        input_kernel, shape(D, TOK, dtype=F32), [], 1 << 20, "input_grad", *dh1_parts, x_own, d_mid, gains
    )
    gains_grad, q_grad, k_grad, v_grad, o_grad = call(
        attn_grads_kernel,
        (shape(2, ROWS, dtype=F32), shape(ROWS, D, dtype=F32), shape(ROWS, 320, dtype=F32),
         shape(ROWS, 320, dtype=F32), shape(ROWS, D, dtype=F32)),
        [pltpu.VMEM((CTX, PADDED, 512), F32)],
        1 << 20,
        "attn_grads",
        *at_pieces,
    )
    return (
        hidden_out.T, in_grad.T, gains_grad, q_grad, k_grad, v_grad, o_grad, gate_grad, up_grad, down_grad
    )


def solution(mesh):
    tokens = P(("dp", "ctx"), None)
    rows = P("dp", None)
    gains = P(None, "dp")
    return jax.shard_map(
        on_device,
        mesh=mesh,
        in_specs=(tokens, tokens, gains) + (rows,) * 7,
        out_specs=(tokens, tokens, gains) + (rows,) * 7,
        check_vma=False,
    )
```
